128 devices in a mesh: grp: 8 (over x, core), hub: 16 (over y, z).
Axes of the slice: x: 4, y: 4, z: 4, core: 2. Of those that a mesh axis runs over, the one named last changes fastest.
Arguments:
- embed: bfloat16 [1048576, 128], P(('grp', 'hub')), may hold values from -6 to 6
- hub_ids: int32 [128, 4], P(('grp', 'hub')), may hold values from 0 to 63
- send_ids: int32 [128, 8, 4], P(('grp', 'hub')), may hold values from 0 to 63
- tile_row: int32 [128, 192], P(('grp', 'hub')), may hold values from 0 to 63
- tile_col: int32 [128, 192], P(('grp', 'hub')), may hold values from 0 to 159
- tile_val: bfloat16 [24576, 128, 128], P(('grp', 'hub')), may hold values from -0.3125 to 0.3125
- tile_count: int32 [128], P(('grp', 'hub')), may hold values from 96 to 192, as said below
Outputs:
- spectral: float32 [1048576, 128], P(('grp', 'hub'))
The draws below stay inside these ranges and needn't reach their ends.
Inputs may be any that keep to these rules, and one draw needn't show every extreme that they name: `tile_count`: each device has at least 96 live tile slots and some device has all 192 live; slots at or past a device's count are ignored.
All inputs are finite; a program needn't handle non-finite values.
Results may differ from the reference program's by a relative error of at most 0.0051.
Values may be sent and summed in bfloat16 or wider, within the bound.
A program may use at most 128 MiB of HBM per device.

```python
import math
import jax
import jax.numpy as jnp
import numpy as np
from jax import lax

EMB = 128
BLK = 128
NB_DEV = 64
TILES = 192
HUB_DEV = 4
TAIL_K = 4
ORDER = 4
NODES = 1048576
COLS = 160
N_GRP = 8
N_HUB = 16
DEVICES = 128


def draw_tile_count(key, part):
    counts = jax.random.randint(key, (DEVICES,), TILES // 2, TILES + 1, dtype=jnp.int32)
    position = jax.random.randint(jax.random.fold_in(key, 7), (), 0, DEVICES, dtype=jnp.int32)
    return jnp.where(jnp.arange(DEVICES, dtype=jnp.int32) == position, TILES, counts).astype(jnp.int32)


def touch_ends(entries, own_key, smallest, top_value):
    spot = [jax.random.randint(jax.random.fold_in(own_key, axis), (), 0, length) for axis, length in enumerate(entries.shape)]
    widest = entries.shape.index(max(entries.shape))
    neighbour = spot[:widest] + [(spot[widest] + 1) % entries.shape[widest]] + spot[widest + 1:]
    return entries.at[tuple(spot)].set(smallest).at[tuple(neighbour)].set(top_value)


def block_levels(own_key, extent, cuts, smallest, top_value):
    level = 1.0
    for axis_at, parts in cuts:
        draws = jax.random.uniform(jax.random.fold_in(jax.random.fold_in(own_key, 6), axis_at), (parts,), jnp.float32, smallest / len(cuts), top_value / len(cuts))
        level = level * jnp.repeat(jnp.exp(draws), extent[axis_at] // parts).reshape((-1,) + (1,) * (len(extent) - 1 - axis_at))
    return level


def rank_table(number_of, lean):
    weights = [(1 << 20) // math.isqrt(rank ** lean) + 1 for rank in range(1, number_of + 1)]
    spread = 1 + sum(weights) // (1 << 30)
    return np.cumsum(np.array([max(1, weight // spread) for weight in weights]))


def ranked(stream_key, shape, count, lean):
    grid = rank_table(count, lean)
    ticket = jax.random.randint(jax.random.fold_in(stream_key, 1), shape, 0, int(grid[count - 1]))
    grade = jnp.searchsorted(jnp.asarray(grid, jnp.int32), ticket, side="right")
    return jax.random.permutation(jax.random.fold_in(stream_key, 2), count)[grade].astype(jnp.int32)


def normal_values(rng, shape, spread, reach, split=(), kind=jnp.bfloat16):
    entries = jax.random.normal(rng, shape, jnp.float32) * spread
    if len(split) > 0:
        entries = block_levels(rng, shape, split, -0.22, 0.18) * entries
    return jnp.clip(entries, min=-reach, max=reach).astype(kind)


def setup_inputs(seed: int = 0) -> dict:
    streams_of = jax.random.split(jax.random.key(seed), 8)
    embed = normal_values(streams_of[0], (NODES, EMB), 1.0, 6.0, ((0, 128),))
    hub_ids = touch_ends(jax.random.randint(streams_of[1], (DEVICES, HUB_DEV), 0, NB_DEV), jax.random.fold_in(streams_of[1], 1), 0, NB_DEV - 1).astype(jnp.int32)
    send_ids = touch_ends(jax.random.randint(streams_of[2], (DEVICES, N_GRP, TAIL_K), 0, NB_DEV), jax.random.fold_in(streams_of[2], 1), 0, NB_DEV - 1).astype(jnp.int32)
    tile_row = touch_ends(jax.random.randint(streams_of[3], (DEVICES, TILES), 0, NB_DEV), jax.random.fold_in(streams_of[3], 1), 0, NB_DEV - 1).astype(jnp.int32)
    tile_col = touch_ends(ranked(streams_of[4], (DEVICES, TILES), COLS, 2), jax.random.fold_in(streams_of[4], 3), 0, COLS - 1).astype(jnp.int32)
    tile_val = normal_values(streams_of[5], (DEVICES * TILES, BLK, BLK), (BLK * TILES // NB_DEV) ** -0.5, 0.3125, ((0, 128),))
    tile_count = draw_tile_count(jax.random.fold_in(streams_of[7], 71), 0)
    return dict(embed=embed, hub_ids=hub_ids, send_ids=send_ids, tile_row=tile_row, tile_col=tile_col, tile_val=tile_val, tile_count=tile_count)


SHIFT = 0.2
THETA = 3.0


def bessel_scaled(order_index):
    total = 0.0
    for term in range(40):
        total += (THETA / 2.0) ** (2 * term + order_index) / (math.factorial(term) * math.factorial(term + order_index))
    return math.exp(-THETA) * total


def coefficients():
    values = [bessel_scaled(0)]
    for order_index in range(1, ORDER + 1):
        values.append(2.0 * ((-1.0) ** order_index) * bessel_scaled(order_index))
    return values


def reference(embed, hub_ids, send_ids, tile_row, tile_col, tile_val, tile_count):
    tiles = tile_val.reshape(DEVICES, TILES, BLK, BLK)
    block_range = jnp.arange(NB_DEV, dtype=jnp.int32)
    slot_range = jnp.arange(TILES, dtype=jnp.int32)

    def apply(field):
        blocks = field.reshape(DEVICES * NB_DEV, BLK, EMB)
        owned = field.reshape(DEVICES, NB_DEV * BLK, EMB)

        def one_device(device):
            group = device // N_HUB
            column = device % N_HUB
            peers = group * N_HUB + jnp.arange(N_HUB, dtype=jnp.int32)
            hub_glob = (peers[:, None] * NB_DEV + hub_ids[peers]).reshape(-1)
            owners = jnp.arange(N_GRP, dtype=jnp.int32) * N_HUB + column
            tail_glob = (owners[:, None] * NB_DEV + send_ids[owners, group]).reshape(-1)
            local_glob = device * NB_DEV + block_range
            glob = jnp.concatenate([local_glob, hub_glob, tail_glob]).astype(jnp.int32)
            space = blocks[glob]
            picked = space[tile_col[device]]
            prod = jnp.einsum("tij,tjk->tik", tiles[device].astype(jnp.float32), picked.astype(jnp.float32), precision=lax.Precision.HIGHEST)
            live = (slot_range < tile_count[device]).astype(jnp.float32)
            masked = prod * live[:, None, None]
            summed = jax.ops.segment_sum(masked, tile_row[device], num_segments=NB_DEV)
            return summed.reshape(NB_DEV * BLK, EMB) - SHIFT * owned[device].astype(jnp.float32)

        return lax.map(one_device, jnp.arange(DEVICES, dtype=jnp.int32)).reshape(NODES, EMB)

    weights = coefficients()
    previous = embed
    spectral = weights[0] * previous.astype(jnp.float32)
    current = apply(previous).astype(jnp.bfloat16)
    spectral = spectral + weights[1] * current.astype(jnp.float32)
    for order_index in range(2, ORDER + 1):
        following = (2.0 * apply(current) - previous.astype(jnp.float32)).astype(jnp.bfloat16)
        spectral = spectral + weights[order_index] * following.astype(jnp.float32)
        previous, current = current, following
    return spectral
```

```python
import functools
import math

import jax
import jax.numpy as jnp
from jax import lax
from jax.experimental import pallas as pl
from jax.experimental.pallas import tpu as pltpu
from jax.sharding import PartitionSpec as P

ORDER = 4
SHIFT = 0.2
THETA = 3.0
MESH = pl.DeviceIdType.MESH

NB = 64
TILES = 192
HUB0 = 64
TAIL0 = 128
COLS = 160
BLK = 128
EMB = 128
UNROLL = 8

TAILS = ((2, 0), (2, 1), (1, 0), (1, 1), (3, 0), (3, 1), (0, 1))
NAMES = ("m1p", "m1m", "m2p", "m2m")
for _q in (0, -1, 1):
    NAMES += tuple(f"{s}{_q}" for s in ("s1p", "s1m", "s2p", "s2m"))
NAMES += ("s1p2a", "s1p2b", "s1m2a", "s1m2b", "s2p2", "s2m2")
NHUB = len(NAMES)
NMSG = 2 * NHUB + len(TAILS)


def bessel_scaled(order_index):
    total = 0.0
    for term in range(40):
        total += (THETA / 2.0) ** (2 * term + order_index) / (
            math.factorial(term) * math.factorial(term + order_index)
        )
    return math.exp(-THETA) * total


def coefficients():
    values = [bessel_scaled(0)]
    for order_index in range(1, ORDER + 1):
        values.append(2.0 * (-1.0) ** order_index * bessel_scaled(order_index))
    return values


def kernel(
    cols, prev, last, hub_ids, send_ids, embed, tile_val, out,
    sp0, sp1, sp2, sp3, start, tiles, sums, outgoing, load_sem, tile_sem, send_sem, recv_sem,
):
    spaces = (sp0, sp1, sp2, sp3)
    coef = coefficients()
    grp = lax.axis_index("grp")
    hub = lax.axis_index("hub")
    x, core = grp // 2, grp % 2
    y, z = hub // 4, hub % 4

    load0 = pltpu.make_async_copy(embed, start, load_sem.at[0])
    load0.start()
    load1 = pltpu.make_async_copy(embed, sp0.at[pl.ds(0, NB)], load_sem.at[1])
    load1.start()
    quarter = TILES // 4
    loads = []
    for part in range(4):
        cut = pl.ds(part * quarter, quarter)
        loads.append(pltpu.make_async_copy(tile_val.at[cut], tiles.at[cut], tile_sem.at[part]))
        loads[-1].start()

    def place(fam, d1, d2):
        dy, dz = (d2, d1) if fam == 0 else (d1, d2)
        return ((y + dy + 4) % 4) * 4 + (z + dz + 4) % 4

    def tail_group(dx, dc):
        return ((x + dx) % 4) * 2 + (core + dc) % 2

    barrier = pltpu.get_barrier_semaphore()
    friends = [(grp, place(0, d1, d2)) for d1, d2 in ((1, 0), (-1, 0), (0, 1), (0, -1))]
    friends += [(tail_group(dx, dc), hub) for dx, dc in TAILS]
    for friend in friends:
        pl.semaphore_signal(barrier, inc=1, device_id=friend, device_id_type=MESH)

    plan = {
        "m1p": ((0, 0), 0, 2, (1, 0)),
        "m1m": ((0, 0), 0, 2, (-1, 0)),
        "m2p": ((-1, 0), 0, 1, (1, 0)),
        "m2m": ((1, 0), 1, 1, (-1, 0)),
    }
    for q in (0, -1, 1):
        plan[f"s1p{q}"] = ((q, 0), 0, 2, (0, 1))
        plan[f"s1m{q}"] = ((q, 0), 0, 2, (0, -1))
    plan["s1p2a"] = ((2, 0), 0, 1, (0, 1))
    plan["s1p2b"] = ((2, 0), 1, 1, (0, 1))
    plan["s1m2a"] = ((2, 0), 0, 1, (0, -1))
    plan["s1m2b"] = ((2, 0), 1, 1, (0, -1))
    for q in (0, -1, 1, 2):
        plan[f"s2p{q}"] = ((q, -1), 0, 1, (0, 1))
        plan[f"s2m{q}"] = ((q, 1), 1, 1, (0, -1))

    def hub_copy(step, fam, name, arriving=False):
        (r1, r2), first, count, (t1, t2) = plan[name]
        if arriving:
            r1, r2 = r1 - t1, r2 - t2
        r1, r2 = (r1 + 8) % 4, (r2 + 8) % 4
        region = pl.ds(HUB0 + place(fam, r1, r2) * 4 + fam * 2 + first, count)
        ident = fam * NHUB + NAMES.index(name)
        return pltpu.make_async_remote_copy(
            src_ref=spaces[step].at[region],
            dst_ref=spaces[step].at[region],
            send_sem=send_sem.at[step, ident],
            recv_sem=recv_sem.at[step, ident],
            device_id=(grp, place(fam, t1, t2)),
            device_id_type=MESH,
        )

    def tail_copy(step, number, arriving=False):
        dx, dc = TAILS[number]
        target = tail_group(dx, dc)
        source = tail_group(4 - dx, dc) if arriving else grp
        ident = 2 * NHUB + number
        return pltpu.make_async_remote_copy(
            src_ref=outgoing.at[pl.ds(target * 4, 4)],
            dst_ref=spaces[step].at[pl.ds(TAIL0 + source * 4, 4)],
            send_sem=send_sem.at[step, ident],
            recv_sem=recv_sem.at[step, ident],
            device_id=(target, hub),
            device_id_type=MESH,
        )

    def row_of(step, row):
        if step == 0:
            return start[row]
        value = sums[last[row]] - SHIFT * spaces[step - 1][row].astype(jnp.float32)
        if step >= 2:
            value = 2.0 * value - spaces[step - 2][row].astype(jnp.float32)
        return value.astype(jnp.bfloat16)

    sums[TILES] = jnp.zeros((BLK, EMB), jnp.float32)
    load0.wait()
    pl.semaphore_wait(barrier, len(friends))

    for step in range(ORDER):
        space = spaces[step]

        def go(name):
            for fam in (0, 1):
                hub_copy(step, fam, name).start()

        def pass_on(name, *then):
            for fam in (0, 1):
                hub_copy(step, fam, name, arriving=True).wait_recv()
                for other in then:
                    hub_copy(step, fam, other).start()

        for slot in range(4):
            space[HUB0 + hub * 4 + slot] = row_of(step, hub_ids[slot])
        for name in ("m1p", "m1m", "s1p0", "s1m0"):
            go(name)
        for number, (dx, dc) in enumerate(TAILS):
            target = tail_group(dx, dc)

            def export(slot, carry):
                outgoing[target * 4 + slot] = row_of(step, send_ids[target * 4 + slot])
                return carry

            lax.fori_loop(0, 4, export, 0)
            tail_copy(step, number).start()

        def keep_tail(slot, carry):
            space[TAIL0 + grp * 4 + slot] = row_of(step, send_ids[grp * 4 + slot])
            return carry

        lax.fori_loop(0, 4, keep_tail, 0)

        def own(row, carry):
            if step == 0:
                value = start[row]
                out[row] = coef[0] * value.astype(jnp.float32)
            else:
                value = row_of(step, row)
                space[row] = value
                out[row] = out[row] + coef[step] * value.astype(jnp.float32)
            return carry

        lax.fori_loop(0, NB, own, 0)

        pass_on("m1p", "m2p")
        pass_on("m1m", "m2m")
        for name in ("s1p-1", "s1m-1", "s1p1", "s1m1"):
            go(name)
        pass_on("s1p0", "s2p0")
        pass_on("s1m0", "s2m0")
        pass_on("m2p", "s1p2a", "s1m2a")
        pass_on("m2m", "s1p2b", "s1m2b")
        pass_on("s1p-1", "s2p-1")
        pass_on("s1m-1", "s2m-1")
        pass_on("s1p1", "s2p1")
        pass_on("s1m1", "s2m1")
        pass_on("s1p2a", "s2p2")
        pass_on("s1m2b", "s2m2")
        for name in ("s1p2b", "s1m2a", "s2p0", "s2m0", "s2p-1", "s2m-1", "s2p1", "s2m1", "s2p2", "s2m2"):
            pass_on(name)
        for number in range(len(TAILS)):
            tail_copy(step, number, arriving=True).wait_recv()
        for number in range(len(TAILS)):
            tail_copy(step, number).wait_send()
        for fam in (0, 1):
            for name in NAMES:
                hub_copy(step, fam, name).wait_send()
        if step == 0:
            load1.wait()
            for load in loads:
                load.wait()

        def multiply(group, carry):
            for inner in range(UNROLL):
                slot = group * UNROLL + inner
                product = jnp.dot(tiles[slot], space[cols[slot]], preferred_element_type=jnp.float32)
                sums[slot] = sums[prev[slot]] + product
            return carry

        lax.fori_loop(0, TILES // UNROLL, multiply, 0)

    def finish(row, carry):
        value = row_of(ORDER, row)
        out[row] = out[row] + coef[ORDER] * value.astype(jnp.float32)
        return carry

    lax.fori_loop(0, NB, finish, 0)


def shards(embed, hub_ids, send_ids, tile_row, tile_col, tile_val, tile_count):
    slots = jnp.arange(TILES, dtype=jnp.int32)
    rows = tile_row[0]
    key = jnp.where(slots < tile_count[0], rows, -1)
    seen = jnp.where((key[None, :] == rows[:, None]) & (slots[None, :] < slots[:, None]), slots[None, :], -1)
    prev = jnp.max(seen, axis=1)
    prev = jnp.where(prev < 0, TILES, prev)
    blocks = jnp.arange(NB, dtype=jnp.int32)
    last = jnp.max(jnp.where(key[None, :] == blocks[:, None], slots[None, :], -1), axis=1)
    last = jnp.where(last < 0, TILES, last)

    smem = pl.BlockSpec(memory_space=pltpu.SMEM)
    hbm = pl.BlockSpec(memory_space=pl.ANY)
    out = pl.pallas_call(
        kernel,
        out_shape=jax.ShapeDtypeStruct((NB, BLK, EMB), jnp.float32),
        in_specs=[smem] * 5 + [hbm] * 2,
        out_specs=pl.BlockSpec(memory_space=pltpu.VMEM),
        scratch_shapes=[pltpu.VMEM((COLS, BLK, EMB), jnp.bfloat16)] * 4
        + [
            pltpu.VMEM((NB, BLK, EMB), jnp.bfloat16),
            pltpu.VMEM((TILES, BLK, BLK), jnp.bfloat16),
            pltpu.VMEM((TILES + 1, BLK, EMB), jnp.float32),
            pltpu.VMEM((32, BLK, EMB), jnp.bfloat16),
            pltpu.SemaphoreType.DMA((2,)),
            pltpu.SemaphoreType.DMA((4,)),
            pltpu.SemaphoreType.DMA((ORDER, NMSG)),
            pltpu.SemaphoreType.DMA((ORDER, NMSG)),
        ],
        compiler_params=pltpu.CompilerParams(
            collective_id=0, has_side_effects=True, vmem_limit_bytes=60 * 1024 * 1024
        ),
    )(
        tile_col[0], prev, last, hub_ids[0], send_ids[0].reshape(-1),
        embed.reshape(NB, BLK, EMB), tile_val,
    )
    return out.reshape(NB * BLK, EMB)


def solution(mesh):
    both = ("grp", "hub")
    return jax.shard_map(
        shards,
        mesh=mesh,
        in_specs=(
            P(both, None), P(both, None), P(both, None, None), P(both, None),
            P(both, None), P(both, None, None), P(both),
        ),
        out_specs=P(both, None),
        check_vma=False,
    )
```

```python
import functools
import math

import jax
import jax.numpy as jnp
from jax import lax
from jax.experimental import pallas as pl
from jax.experimental.pallas import tpu as pltpu
from jax.sharding import PartitionSpec as P

ORDER = 4
SHIFT = 0.2
THETA = 3.0
MESH = pl.DeviceIdType.MESH

NB = 64
TILES = 192
HUB0 = 64
TAIL0 = 128
COLS = 160
BLK = 128
EMB = 128
UNROLL = 48

TAILS = ((2, 0), (2, 1), (1, 0), (1, 1), (3, 0), (3, 1), (0, 1))
PLAN = {
    "m1p": ((0, 0), 0, 2, (1, 0)),
    "m1m": ((0, 0), 0, 2, (-1, 0)),
    "m1d": ((0, 0), 0, 2, (2, 0)),
}
for _q in (0, -1, 1):
    PLAN[f"s1p{_q}"] = ((_q, 0), 0, 2, (0, 1))
    PLAN[f"s1m{_q}"] = ((_q, 0), 0, 2, (0, -1))
    PLAN[f"s2p{_q}"] = ((_q, -1), 0, 1, (0, 1))
    PLAN[f"s2m{_q}"] = ((_q, 1), 1, 1, (0, -1))
PLAN["s1p2"] = ((2, 0), 0, 2, (0, 1))
PLAN["s1m2"] = ((2, 0), 0, 2, (0, -1))
PLAN["s1d2"] = ((2, 0), 0, 2, (0, 2))
NAMES = tuple(PLAN)
NHUB = len(NAMES)
NMSG = 2 * NHUB + len(TAILS)


def bessel_scaled(order_index):
    total = 0.0
    for term in range(40):
        total += (THETA / 2.0) ** (2 * term + order_index) / (
            math.factorial(term) * math.factorial(term + order_index)
        )
    return math.exp(-THETA) * total


def coefficients():
    values = [bessel_scaled(0)]
    for order_index in range(1, ORDER + 1):
        values.append(2.0 * (-1.0) ** order_index * bessel_scaled(order_index))
    return values


def kernel(
    count_hbm, cols_hbm, hub_hbm, send_hbm, row_hbm, embed, tile_val, out,
    sp0, sp1, sp2, sp3, start, tiles, sums, outgoing,
    prev_made, last_made, prev, last, count, cols, hub_ids, send_ids, tile_row, small_sem, table_sem, load_sem, tile_sem, send_sem, recv_sem,
):
    spaces = (sp0, sp1, sp2, sp3)
    coef = coefficients()
    grp = lax.axis_index("grp")
    hub = lax.axis_index("hub")
    x, core = grp // 2, grp % 2
    y, z = hub // 4, hub % 4

    load0 = pltpu.make_async_copy(embed, start, load_sem.at[0])
    load0.start()
    small = [
        pltpu.make_async_copy(there, here, small_sem.at[number])
        for number, (there, here) in enumerate(
            ((hub_hbm, hub_ids), (send_hbm, send_ids), (count_hbm, count), (row_hbm, tile_row), (cols_hbm, cols))
        )
    ]
    for part in small:
        part.start()
    load1 = pltpu.make_async_copy(embed, sp0.at[pl.ds(0, NB)], load_sem.at[1])
    quarter = TILES // 4
    loads = []
    for part in range(4):
        cut = pl.ds(part * quarter, quarter)
        loads.append(pltpu.make_async_copy(tile_val.at[cut], tiles.at[cut], tile_sem.at[part]))

    def place(fam, d1, d2):
        dy, dz = (d2, d1) if fam == 0 else (d1, d2)
        return ((y + dy + 4) % 4) * 4 + (z + dz + 4) % 4

    def tail_group(dx, dc):
        return ((x + dx) % 4) * 2 + (core + dc) % 2

    barrier = pltpu.get_barrier_semaphore()
    friends = [(grp, place(0, d1, d2)) for d1, d2 in ((1, 0), (-1, 0), (2, 0), (0, 1), (0, -1), (0, 2))]
    friends += [(tail_group(dx, dc), hub) for dx, dc in TAILS]
    for friend in friends:
        pl.semaphore_signal(barrier, inc=1, device_id=friend, device_id_type=MESH)

    def hub_copy(step, fam, name, arriving=False):
        (r1, r2), first, count, (t1, t2) = PLAN[name]
        if arriving:
            r1, r2 = r1 - t1, r2 - t2
        r1, r2 = (r1 + 8) % 4, (r2 + 8) % 4
        region = pl.ds(HUB0 + place(fam, r1, r2) * 4 + fam * 2 + first, count)
        ident = fam * NHUB + NAMES.index(name)
        return pltpu.make_async_remote_copy(
            src_ref=spaces[step].at[region],
            dst_ref=spaces[step].at[region],
            send_sem=send_sem.at[ident],
            recv_sem=recv_sem.at[step % 2, ident],
            device_id=(grp, place(fam, t1, t2)),
            device_id_type=MESH,
        )

    def tail_copy(step, number, arriving=False):
        dx, dc = TAILS[number]
        target = tail_group(dx, dc)
        source = tail_group(4 - dx, dc) if arriving else grp
        ident = 2 * NHUB + number
        return pltpu.make_async_remote_copy(
            src_ref=outgoing.at[pl.ds(target * 4, 4)],
            dst_ref=spaces[step].at[pl.ds(TAIL0 + source * 4, 4)],
            send_sem=send_sem.at[ident],
            recv_sem=recv_sem.at[step % 2, ident],
            device_id=(target, hub),
            device_id_type=MESH,
        )

    def row_of(step, row):
        if step == 0:
            return start[row]
        value = sums[last[0, row]] - SHIFT * spaces[step - 1][row].astype(jnp.float32)
        if step >= 2:
            value = 2.0 * value - spaces[step - 2][row].astype(jnp.float32)
        return value.astype(jnp.bfloat16)

    prev_copy = pltpu.make_async_copy(prev_made, prev, table_sem.at[0])
    last_copy = pltpu.make_async_copy(last_made, last, table_sem.at[1])

    def tables():
        across = lax.broadcasted_iota(jnp.int32, (TILES, TILES), 1)
        down = lax.broadcasted_iota(jnp.int32, (TILES, TILES), 0)
        rows = jnp.broadcast_to(tile_row[...], (TILES, TILES))
        live = jnp.where(across < count[0], rows, -1)
        key = jnp.sum(jnp.where(across == down, live, 0), axis=1, keepdims=True)
        before = jnp.max(jnp.where((key == rows) & (down < across), down, -1), axis=0, keepdims=True)
        prev_made[...] = jnp.where(before < 0, TILES, before)
        found = jnp.max(jnp.where(key == across[:, :BLK], down[:, :BLK], -1), axis=0, keepdims=True)
        last_made[...] = jnp.where(found < 0, TILES, found)
        prev_copy.start()
        last_copy.start()

    sums[TILES] = jnp.zeros((BLK, EMB), jnp.float32)
    for part in small:
        part.wait()
    load0.wait()
    pl.semaphore_wait(barrier, len(friends))

    for step in range(ORDER):
        space = spaces[step]

        def go(name):
            for fam in (0, 1):
                hub_copy(step, fam, name).start()

        def pass_on(name, *then):
            for fam in (0, 1):
                hub_copy(step, fam, name, arriving=True).wait_recv()
                for other in then:
                    hub_copy(step, fam, other).start()

        for slot in range(4):
            space[HUB0 + hub * 4 + slot] = row_of(step, hub_ids[0, slot])
        for name in ("m1p", "m1m", "m1d", "s1p0", "s1m0"):
            go(name)
        for number, (dx, dc) in enumerate(TAILS):
            target = tail_group(dx, dc)

            def export(slot, carry):
                outgoing[target * 4 + slot] = row_of(step, send_ids[0, slot, target])
                return carry

            lax.fori_loop(0, 4, export, 0, unroll=True)
            tail_copy(step, number).start()

        def keep_tail(slot, carry):
            space[TAIL0 + grp * 4 + slot] = row_of(step, send_ids[0, slot, grp])
            return carry

        lax.fori_loop(0, 4, keep_tail, 0, unroll=True)

        if step == 0:
            load1.start()
            for part in loads:
                part.start()
            tables()

        def own(pair, carry):
            for inner in range(2):
                row = pair * 2 + inner
                if step == 0:
                    out[row] = coef[0] * start[row].astype(jnp.float32)
                else:
                    value = row_of(step, row)
                    space[row] = value
                    out[row] = out[row] + coef[step] * value.astype(jnp.float32)
            return carry

        lax.fori_loop(0, NB // 4, own, 0)
        pass_on("m1p")
        pass_on("m1m")
        for name in ("s1p-1", "s1m-1", "s1p1", "s1m1"):
            go(name)
        lax.fori_loop(NB // 4, NB // 2, own, 0)
        pass_on("m1d", "s1d2", "s1p2", "s1m2")
        pass_on("s1p0", "s2p0")
        pass_on("s1m0", "s2m0")
        for q in (-1, 1):
            pass_on(f"s1p{q}", f"s2p{q}")
            pass_on(f"s1m{q}", f"s2m{q}")
        for name in ("s1p2", "s1m2", "s1d2", "s2p0", "s2m0", "s2p-1", "s2m-1", "s2p1", "s2m1"):
            pass_on(name)
        for number in range(len(TAILS)):
            tail_copy(step, number, arriving=True).wait_recv()
        for number in range(len(TAILS)):
            tail_copy(step, number).wait_send()
        for fam in (0, 1):
            for name in NAMES:
                hub_copy(step, fam, name).wait_send()
        if step == 0:
            load1.wait()
            for part in loads:
                part.wait()
            prev_copy.wait()
            last_copy.wait()

        def multiply(group, carry):
            for inner in range(UNROLL):
                slot = group * UNROLL + inner
                product = jnp.dot(tiles[slot], space[cols[0, slot]], preferred_element_type=jnp.float32)
                sums[slot] = sums[prev[0, slot]] + product
            return carry

        lax.fori_loop(0, TILES // UNROLL, multiply, 0)

    def finish(pair, carry):
        for inner in range(2):
            row = pair * 2 + inner
            value = row_of(ORDER, row).astype(jnp.float32)
            out[row] = out[row] + coef[ORDER] * value
        return carry

    lax.fori_loop(0, NB // 2, finish, 0)


def shards(embed, hub_ids, send_ids, tile_row, tile_col, tile_val, tile_count):
    hbm = pl.BlockSpec(memory_space=pl.ANY)
    out = pl.pallas_call(
        kernel,
        out_shape=pltpu.VMEM((NB, BLK, EMB), jnp.float32),
        in_specs=[hbm] * 7,
        out_specs=pl.BlockSpec(memory_space=pltpu.VMEM),
        scratch_shapes=[pltpu.VMEM((COLS, BLK, EMB), jnp.bfloat16)] * 4
        + [
            pltpu.VMEM((NB, BLK, EMB), jnp.bfloat16),
            pltpu.VMEM((TILES, BLK, BLK), jnp.bfloat16),
            pltpu.VMEM((TILES + 1, BLK, EMB), jnp.float32),
            pltpu.VMEM((32, BLK, EMB), jnp.bfloat16),
            pltpu.VMEM((1, TILES), jnp.int32),
            pltpu.VMEM((1, BLK), jnp.int32),
            pltpu.SMEM((1, TILES), jnp.int32),
            pltpu.SMEM((1, BLK), jnp.int32),
            pltpu.SMEM((1,), jnp.int32),
            pltpu.SMEM((1, TILES), jnp.int32),
            pltpu.SMEM((1, 4), jnp.int32),
            pltpu.SMEM((1, 4, 8), jnp.int32),
            pltpu.VMEM((1, TILES), jnp.int32),
            pltpu.SemaphoreType.DMA((5,)),
            pltpu.SemaphoreType.DMA((2,)),
            pltpu.SemaphoreType.DMA((2,)),
            pltpu.SemaphoreType.DMA((4,)),
            pltpu.SemaphoreType.DMA((NMSG,)),
            pltpu.SemaphoreType.DMA((2, NMSG)),
        ],
        compiler_params=pltpu.CompilerParams(
            collective_id=0, has_side_effects=True, vmem_limit_bytes=56 * 1024 * 1024
        ),
    )(
        tile_count, tile_col, hub_ids, jnp.swapaxes(send_ids, 1, 2), tile_row,
        embed.reshape(NB, BLK, EMB), tile_val,
    )
    return out.reshape(NB * BLK, EMB)


def solution(mesh):
    both = ("grp", "hub")
    return jax.shard_map(
        shards,
        mesh=mesh,
        in_specs=(
            P(both, None), P(both, None), P(both, None, None), P(both, None),
            P(both, None), P(both, None, None), P(both),
        ),
        out_specs=P(both, None),
        check_vma=False,
    )
```

```python
import functools
import math

import jax
import jax.numpy as jnp
from jax import lax
from jax.experimental import pallas as pl
from jax.experimental.pallas import tpu as pltpu
from jax.sharding import PartitionSpec as P

ORDER = 4
SHIFT = 0.2
THETA = 3.0
MESH = pl.DeviceIdType.MESH

NB = 64
TILES = 192
HUB0 = 64
TAIL0 = 128
COLS = 160
BLK = 128
EMB = 128
UNROLL = 96

TAILS = ((2, 0), (2, 1), (1, 0), (1, 1), (3, 0), (3, 1), (0, 1))
PLAN = {
    "m1p": ((0, 0), 0, 2, (1, 0)),
    "m1m": ((0, 0), 0, 2, (-1, 0)),
    "m1d": ((0, 0), 0, 2, (2, 0)),
}
for _q in (0, -1, 1):
    PLAN[f"s1p{_q}"] = ((_q, 0), 0, 2, (0, 1))
    PLAN[f"s1m{_q}"] = ((_q, 0), 0, 2, (0, -1))
    PLAN[f"s2p{_q}"] = ((_q, -1), 0, 1, (0, 1))
    PLAN[f"s2m{_q}"] = ((_q, 1), 1, 1, (0, -1))
PLAN["s1p2"] = ((2, 0), 0, 2, (0, 1))
PLAN["s1m2"] = ((2, 0), 0, 2, (0, -1))
PLAN["s1d2"] = ((2, 0), 0, 2, (0, 2))
NAMES = tuple(PLAN)
NHUB = len(NAMES)
NMSG = 2 * NHUB + len(TAILS)


def bessel_scaled(order_index):
    total = 0.0
    for term in range(40):
        total += (THETA / 2.0) ** (2 * term + order_index) / (
            math.factorial(term) * math.factorial(term + order_index)
        )
    return math.exp(-THETA) * total


def coefficients():
    values = [bessel_scaled(0)]
    for order_index in range(1, ORDER + 1):
        values.append(2.0 * (-1.0) ** order_index * bessel_scaled(order_index))
    return values


def kernel(
    count_hbm, cols_hbm, hub_hbm, send_hbm, row_hbm, embed, tile_val, out,
    sp0, sp1, sp2, sp3, start, tiles, sums, outgoing,
    prev_made, last_made, prev, last, count, cols, hub_ids, send_ids, tile_row, small_sem, table_sem, load_sem, tile_sem, send_sem, recv_sem,
):
    spaces = (sp0, sp1, sp2, sp3)
    coef = coefficients()
    grp = lax.axis_index("grp")
    hub = lax.axis_index("hub")
    x, core = grp // 2, grp % 2
    y, z = hub // 4, hub % 4

    load0 = pltpu.make_async_copy(embed, start, load_sem.at[0])
    load0.start()
    small = [
        pltpu.make_async_copy(there, here, small_sem.at[number])
        for number, (there, here) in enumerate(
            ((hub_hbm, hub_ids), (send_hbm, send_ids), (count_hbm, count), (row_hbm, tile_row), (cols_hbm, cols))
        )
    ]
    for part in small:
        part.start()
    load1 = pltpu.make_async_copy(embed, sp0.at[pl.ds(0, NB)], load_sem.at[1])
    quarter = TILES // 4
    loads = []
    for part in range(4):
        cut = pl.ds(part * quarter, quarter)
        loads.append(pltpu.make_async_copy(tile_val.at[cut], tiles.at[cut], tile_sem.at[part]))

    def place(fam, d1, d2):
        dy, dz = (d2, d1) if fam == 0 else (d1, d2)
        return ((y + dy + 4) % 4) * 4 + (z + dz + 4) % 4

    def tail_group(dx, dc):
        return ((x + dx) % 4) * 2 + (core + dc) % 2

    barrier = pltpu.get_barrier_semaphore()
    friends = [(grp, place(0, d1, d2)) for d1, d2 in ((1, 0), (-1, 0), (2, 0), (0, 1), (0, -1), (0, 2))]
    friends += [(tail_group(dx, dc), hub) for dx, dc in TAILS]
    for friend in friends:
        pl.semaphore_signal(barrier, inc=1, device_id=friend, device_id_type=MESH)

    def hub_copy(step, fam, name, arriving=False):
        (r1, r2), first, count, (t1, t2) = PLAN[name]
        if arriving:
            r1, r2 = r1 - t1, r2 - t2
        r1, r2 = (r1 + 8) % 4, (r2 + 8) % 4
        region = pl.ds(HUB0 + place(fam, r1, r2) * 4 + fam * 2 + first, count)
        ident = fam * NHUB + NAMES.index(name)
        return pltpu.make_async_remote_copy(
            src_ref=spaces[step].at[region],
            dst_ref=spaces[step].at[region],
            send_sem=send_sem.at[ident],
            recv_sem=recv_sem.at[step % 2, ident],
            device_id=(grp, place(fam, t1, t2)),
            device_id_type=MESH,
        )

    def tail_copy(step, number, arriving=False):
        dx, dc = TAILS[number]
        target = tail_group(dx, dc)
        source = tail_group(4 - dx, dc) if arriving else grp
        ident = 2 * NHUB + number
        return pltpu.make_async_remote_copy(
            src_ref=outgoing.at[pl.ds(target * 4, 4)],
            dst_ref=spaces[step].at[pl.ds(TAIL0 + source * 4, 4)],
            send_sem=send_sem.at[ident],
            recv_sem=recv_sem.at[step % 2, ident],
            device_id=(target, hub),
            device_id_type=MESH,
        )

    def row_of(step, row):
        if step == 0:
            return start[row]
        value = sums[last[0, row]] - SHIFT * spaces[step - 1][row].astype(jnp.float32)
        if step >= 2:
            value = 2.0 * value - spaces[step - 2][row].astype(jnp.float32)
        return value.astype(jnp.bfloat16)

    prev_copy = pltpu.make_async_copy(prev_made, prev, table_sem.at[0])
    last_copy = pltpu.make_async_copy(last_made, last, table_sem.at[1])

    def tables():
        across = lax.broadcasted_iota(jnp.int32, (TILES, TILES), 1)
        down = lax.broadcasted_iota(jnp.int32, (TILES, TILES), 0)
        rows = jnp.broadcast_to(tile_row[...], (TILES, TILES))
        live = jnp.where(across < count[0], rows, -1)
        key = jnp.sum(jnp.where(across == down, live, 0), axis=1, keepdims=True)
        before = jnp.max(jnp.where((key == rows) & (down < across), down, -1), axis=0, keepdims=True)
        prev_made[...] = jnp.where(before < 0, TILES, before)
        found = jnp.max(jnp.where(key == across[:, :BLK], down[:, :BLK], -1), axis=0, keepdims=True)
        last_made[...] = jnp.where(found < 0, TILES, found)
        prev_copy.start()
        last_copy.start()

    sums[TILES] = jnp.zeros((BLK, EMB), jnp.float32)
    for part in small:
        part.wait()
    load0.wait()
    pl.semaphore_wait(barrier, len(friends))

    for step in range(ORDER):
        space = spaces[step]

        def go(name):
            for fam in (0, 1):
                hub_copy(step, fam, name).start()

        def pass_on(name, *then):
            for fam in (0, 1):
                hub_copy(step, fam, name, arriving=True).wait_recv()
                for other in then:
                    hub_copy(step, fam, other).start()

        for slot in range(4):
            space[HUB0 + hub * 4 + slot] = row_of(step, hub_ids[0, slot])
        for name in ("m1p", "m1m", "m1d", "s1p0", "s1m0"):
            go(name)
        for number, (dx, dc) in enumerate(TAILS):
            target = tail_group(dx, dc)

            def export(slot, carry):
                outgoing[target * 4 + slot] = row_of(step, send_ids[0, slot, target])
                return carry

            lax.fori_loop(0, 4, export, 0, unroll=True)
            tail_copy(step, number).start()

        def keep_tail(slot, carry):
            space[TAIL0 + grp * 4 + slot] = row_of(step, send_ids[0, slot, grp])
            return carry

        lax.fori_loop(0, 4, keep_tail, 0, unroll=True)

        if step == 0:
            load1.start()
            for part in loads:
                part.start()
            tables()

        def own(pair, carry):
            for inner in range(2):
                row = pair * 2 + inner
                if step == 0:
                    out[row] = coef[0] * start[row].astype(jnp.float32)
                else:
                    value = row_of(step, row)
                    space[row] = value
                    out[row] = out[row] + coef[step] * value.astype(jnp.float32)
            return carry

        lax.fori_loop(0, NB // 4, own, 0)
        pass_on("m1p")
        pass_on("m1m")
        for name in ("s1p-1", "s1m-1", "s1p1", "s1m1"):
            go(name)
        lax.fori_loop(NB // 4, NB // 2, own, 0)
        pass_on("m1d", "s1d2", "s1p2", "s1m2")
        pass_on("s1p0", "s2p0")
        pass_on("s1m0", "s2m0")
        for q in (-1, 1):
            pass_on(f"s1p{q}", f"s2p{q}")
            pass_on(f"s1m{q}", f"s2m{q}")
        for name in ("s1p2", "s1m2", "s1d2", "s2p0", "s2m0", "s2p-1", "s2m-1", "s2p1", "s2m1"):
            pass_on(name)
        for number in range(len(TAILS)):
            tail_copy(step, number, arriving=True).wait_recv()
        for number in range(len(TAILS)):
            tail_copy(step, number).wait_send()
        for fam in (0, 1):
            for name in NAMES:
                hub_copy(step, fam, name).wait_send()
        if step == 0:
            load1.wait()
            for part in loads:
                part.wait()
            prev_copy.wait()
            last_copy.wait()

        def multiply(group, carry):
            for inner in range(UNROLL):
                slot = group * UNROLL + inner
                product = jnp.dot(tiles[slot], space[cols[0, slot]], preferred_element_type=jnp.float32)
                sums[slot] = sums[prev[0, slot]] + product
            return carry

        lax.fori_loop(0, TILES // UNROLL, multiply, 0)

    def finish(pair, carry):
        for inner in range(2):
            row = pair * 2 + inner
            value = row_of(ORDER, row).astype(jnp.float32)
            out[row] = out[row] + coef[ORDER] * value
        return carry

    lax.fori_loop(0, NB // 2, finish, 0)


def shards(embed, hub_ids, send_ids, tile_row, tile_col, tile_val, tile_count):
    hbm = pl.BlockSpec(memory_space=pl.ANY)
    out = pl.pallas_call(
        kernel,
        out_shape=pltpu.VMEM((NB, BLK, EMB), jnp.float32),
        in_specs=[hbm] * 7,
        out_specs=pl.BlockSpec(memory_space=pltpu.VMEM),
        scratch_shapes=[pltpu.VMEM((COLS, BLK, EMB), jnp.bfloat16)] * 4
        + [
            pltpu.VMEM((NB, BLK, EMB), jnp.bfloat16),
            pltpu.VMEM((TILES, BLK, BLK), jnp.bfloat16),
            pltpu.VMEM((TILES + 1, BLK, EMB), jnp.float32),
            pltpu.VMEM((32, BLK, EMB), jnp.bfloat16),
            pltpu.VMEM((1, TILES), jnp.int32),
            pltpu.VMEM((1, BLK), jnp.int32),
            pltpu.SMEM((1, TILES), jnp.int32),
            pltpu.SMEM((1, BLK), jnp.int32),
            pltpu.SMEM((1,), jnp.int32),
            pltpu.SMEM((1, TILES), jnp.int32),
            pltpu.SMEM((1, 4), jnp.int32),
            pltpu.SMEM((1, 4, 8), jnp.int32),
            pltpu.VMEM((1, TILES), jnp.int32),
            pltpu.SemaphoreType.DMA((5,)),
            pltpu.SemaphoreType.DMA((2,)),
            pltpu.SemaphoreType.DMA((2,)),
            pltpu.SemaphoreType.DMA((4,)),
            pltpu.SemaphoreType.DMA((NMSG,)),
            pltpu.SemaphoreType.DMA((2, NMSG)),
        ],
        compiler_params=pltpu.CompilerParams(
            collective_id=0, has_side_effects=True, vmem_limit_bytes=56 * 1024 * 1024
        ),
    )(
        tile_count, tile_col, hub_ids, jnp.swapaxes(send_ids, 1, 2), tile_row,
        embed.reshape(NB, BLK, EMB), tile_val,
    )
    return out.reshape(NB * BLK, EMB)


def solution(mesh):
    both = ("grp", "hub")
    return jax.shard_map(
        shards,
        mesh=mesh,
        in_specs=(
            P(both, None), P(both, None), P(both, None, None), P(both, None),
            P(both, None), P(both, None, None), P(both),
        ),
        out_specs=P(both, None),
        check_vma=False,
    )
```
